256 devices in a mesh: mp: 2 (over x_hi), lat: 8 (over x_lo, y), lon: 16 (over z, core).
Axes of the slice: x: 4 (x_hi: 2, x_lo: 2; x = x_hi * 2 + x_lo), y: 4, z: 8, core: 2. Of those that a mesh axis runs over, the one named last changes fastest.
Arguments:
- adjoint: float32 [2, 2, 72, 128, 2048], P('mp', None, None, 'lat', 'lon'), may hold values from -6 to 6
- courant: float32 [2, 2, 128, 2048], P('mp', None, 'lat', 'lon'), may hold values from 0.05 to 0.45
- diffusivity: float32 [2, 71, 128, 2048], P('mp', None, 'lat', 'lon'), may hold values from 0.005 to 0.24
- coupling: float32 [2, 128, 2048], P('mp', 'lat', 'lon'), may hold values from 0.05 to 0.45
- partner: int32 [2, 16384], P('mp', ('lat', 'lon')), may hold values from 0 to 16383, as said below
- mask: int32 [2, 128, 2048], P('mp', 'lat', 'lon'), may hold values from 0 to 1, as said below
Outputs:
- result_adjoint: float32 [2, 2, 72, 128, 2048], P('mp', None, None, 'lat', 'lon')
The draws below stay inside these ranges and needn't reach their ends.
Inputs may be any that keep to these rules, and one draw needn't show every extreme that they name: partner[0, q] is the ocean tile coupled to atmosphere tile q and partner[1] is its inverse, tiles numbered as in the first step; the tiles of one device have partners on exactly 64 devices, 2 tiles on each. `mask`: 1 marks a cell over sea; coupled tiles carry the same flags cell by cell.
All inputs are finite; a program needn't handle non-finite values.
Results may differ from the reference program's by a relative error of at most 0.00002.
Values sent between devices are 32-bit elements; how exact they have to be, the bound alone decides.
A program may use at most 64 MiB of HBM per device.

```python
import math
from functools import partial
import jax
import jax.numpy as jnp
from jax import lax

NTR = 2
LEV = 72
TILE = 16
LATB = 16
LONB = 128
STEPS = 4
NLAT = 128
NLON = 2048
TPD = 128
NT = 16384
CAP = 2
N_LAT = 8
N_LON = 16


def pair_tables(key):
    device_count = NT // TPD
    groups_sent = TPD // CAP
    keys_all = jax.random.split(key, 5)
    sources_order = jax.random.permutation(keys_all[0], device_count)
    targets_order = jax.random.permutation(keys_all[1], device_count)
    offsets = jax.random.permutation(keys_all[2], device_count)[:groups_sent]
    sender_perm = jax.vmap(lambda subkey: jax.random.permutation(subkey, TPD))(jax.random.split(keys_all[3], device_count))
    target_perm = jax.vmap(lambda subkey: jax.random.permutation(subkey, TPD))(jax.random.split(keys_all[4], device_count))
    group_index = sender_perm // CAP
    rank_index = sender_perm % CAP
    target = targets_order[(sources_order[:, None] + offsets[group_index]) % device_count]
    local_slot = target_perm[target, group_index * CAP + rank_index]
    forward = (target * TPD + local_slot).reshape(-1).astype(jnp.int32)
    backward = jnp.zeros((NT,), jnp.int32).at[forward].set(jnp.arange(NT, dtype=jnp.int32))
    return (forward, backward)


def draw_partner(key, part):
    forward, backward = pair_tables(jax.random.fold_in(key, 11))
    return jnp.stack([forward, backward])


def tiles_to_grid(tile_flags):
    shaped = tile_flags.reshape(N_LAT, N_LON, LATB, LONB // TILE, TILE)
    return shaped.transpose(0, 2, 1, 3, 4).reshape(NLAT, NLON)


def draw_mask(key, part):
    forward, backward = pair_tables(jax.random.fold_in(key, 11))
    atmos_flags = (jax.random.randint(jax.random.fold_in(key, 23), (NT, TILE), 0, 3) > 0).astype(jnp.int32)
    ocean_flags = atmos_flags[backward]
    return jnp.stack([tiles_to_grid(atmos_flags), tiles_to_grid(ocean_flags)])


def levels(own_key, shape, shards, smallest, top_value):
    factor_of, own = 1.0, jax.random.fold_in(own_key, 6)
    for dim, blocks in shards:
        draws = jnp.exp(jax.random.uniform(jax.random.fold_in(own, dim), (blocks,), jnp.float32, smallest / len(shards), top_value / len(shards)))
        factor_of = factor_of * jnp.repeat(draws, shape[dim] // blocks).reshape([-1 if axis == dim else 1 for axis in range(len(shape))])
    return factor_of


def gaussian(stream_key, shape, scale, limit, cuts=(), held_as=jnp.bfloat16):
    entries = jax.random.normal(stream_key, shape, jnp.float32) * scale
    if len(cuts) > 0:
        entries = levels(stream_key, shape, cuts, -0.22, 0.18) * entries
    return jnp.clip(entries, min=-limit, max=limit).astype(held_as)


def setup_inputs(seed: int = 0) -> dict:
    key_of = jax.random.split(jax.random.key(seed), 7)
    return {
        "adjoint": gaussian(key_of[0], (2, NTR, LEV, NLAT, NLON), 1.0, 6.0, ((0, 2), (3, 8), (4, 16)), jnp.float32),
        "courant": jnp.clip(0.05 + 0.39999999 * jax.random.uniform(key_of[1], (2, 2, NLAT, NLON), jnp.float32) ** levels(key_of[1], (2, 2, NLAT, NLON), ((0, 2), (2, 8), (3, 16)), -0.2, 0.2), 0.05, 0.45),
        "diffusivity": jnp.clip(jnp.exp(math.log(0.24) - 3.871201 * jax.random.uniform(key_of[2], (2, LEV - 1, NLAT, NLON), jnp.float32) ** levels(key_of[2], (2, LEV - 1, NLAT, NLON), ((0, 2), (2, 8), (3, 16)), -0.2, 0.2)), 0.005, 0.24),
        "coupling": jnp.clip(0.05 + 0.39999999 * jax.random.uniform(key_of[3], (2, NLAT, NLON), jnp.float32) ** levels(key_of[3], (2, NLAT, NLON), ((0, 2), (1, 8), (2, 16)), -0.2, 0.2), 0.05, 0.45),
        "partner": draw_partner(jax.random.fold_in(key_of[6], 71), 0),
        "mask": draw_mask(jax.random.fold_in(key_of[6], 71), 0),
    }


def advect(fields, courant_pair):
    zonal = courant_pair[0]
    meridional = courant_pair[1]
    weight = (1.0 - zonal) - meridional
    eastward = zonal * fields
    northward = meridional * fields
    east_next = jnp.roll(eastward, -1, axis=-1)
    north_next = jnp.concatenate([northward[..., 1:, :], jnp.zeros_like(northward[..., :1, :])], axis=-2)
    return (weight * fields + east_next) + north_next


def diffuse(fields, kappa):
    fluxes = kappa * (fields[1:] - fields[:-1])
    edge = jnp.zeros_like(fields[:1])
    return (fields + jnp.concatenate([fluxes, edge], 0)) - jnp.concatenate([edge, fluxes], 0)


def column_step(tracer_fields, courant_pair, kappa):
    return diffuse(advect(tracer_fields, courant_pair), kappa)


def to_tiles(surface):
    tracers = surface.shape[0]
    shaped = surface.reshape(tracers, N_LAT, LATB, N_LON, LONB // TILE, TILE)
    return shaped.transpose(1, 3, 2, 4, 0, 5).reshape(NT, tracers * TILE)


def from_tiles(tile_rows, tracers):
    shaped = tile_rows.reshape(N_LAT, N_LON, LATB, LONB // TILE, tracers, TILE)
    return shaped.transpose(4, 0, 2, 1, 3, 5).reshape(tracers, NLAT, NLON)


def reference(adjoint, courant, diffusivity, coupling, partner, mask):
    fields_all = [adjoint[0], adjoint[1]]
    wet_tiles = [to_tiles(jnp.broadcast_to(mask[model_index].astype(jnp.float32), (NTR, NLAT, NLON))) for model_index in range(2)]
    for step_index in range(STEPS):
        mixed = []
        for model_index in range(2):
            stepper = partial(column_step, courant_pair=courant[model_index], kappa=diffusivity[model_index])
            mixed.append(lax.map(stepper, fields_all[model_index]))
        own = [to_tiles(mixed[model_index][:, 0]) for model_index in range(2)]
        scaled = [to_tiles(coupling[model_index] * mixed[model_index][:, 0]) for model_index in range(2)]
        received = [scaled[1][partner[0]], scaled[0][partner[1]]]
        updated = []
        for model_index in range(2):
            new_tiles = own[model_index] + wet_tiles[model_index] * (received[model_index] - scaled[model_index])
            surface = from_tiles(new_tiles, NTR)
            updated.append(mixed[model_index].at[:, 0].set(surface))
        fields_all = updated
    return jnp.stack(fields_all)
```

```python
import functools

import jax
import jax.numpy as jnp
from jax import lax
from jax.experimental import pallas as pl
from jax.experimental.pallas import tpu as pltpu
from jax.sharding import PartitionSpec as P

TILE = 16
STEPS = 4
MESH = pl.DeviceIdType.MESH
F32 = jnp.float32
BF16 = jnp.bfloat16


def hops(a, b, c):
    return (1 if a else 2) + min(b, 4 - b) + min(c, 8 - c)


OFFSETS = sorted(
    [(a, b, c, d) for a in range(2) for b in range(4) for c in range(8) for d in range(2)],
    key=lambda o: -hops(*o[:3]),
)


def iota(shape, axis):
    return lax.broadcasted_iota(jnp.int32, shape, axis)


def halves(x):
    high = x.astype(BF16)
    low = (x - high.astype(F32)).astype(BF16)
    return high, low


def dot(a, b):
    return jnp.dot(a, b, preferred_element_type=F32)


def joined(x):
    return x[:, :128] + x[:, 128:]


def kernel(
    adj, cour, diff, coup, part, msk, out,
    F, CO, KAP, CP, PT, MK, ST, STW, STS, CZE, CMN, CMS,
    ES, EE, SB, RB, SURF, NROW, BNE, OHP, OHX, LA, LB, KM, CF, ROWS,
    isem, osem, xs, xr, ns, nr, es, er, ts, tr, stage,
):
    mp, lat, lon = lax.axis_index("mp"), lax.axis_index("lat"), lax.axis_index("lon")
    me = lat * 16 + lon
    x_lo, y = lat // 4, lax.rem(lat, 4)
    z, core = lon // 2, lax.rem(lon, 2)
    east, west = (mp, lat, (lon + 1) & 15), (mp, lat, (lon + 15) & 15)
    north, south = (mp, (lat + 1) & 7, lon), (mp, (lat + 7) & 7, lon)

    loads = [
        pltpu.make_async_copy(part, PT, isem.at[0]),
        pltpu.make_async_copy(cour.at[0], CO, isem.at[1]),
        pltpu.make_async_copy(coup.at[0], CP, isem.at[2]),
        pltpu.make_async_copy(diff.at[0], KAP.at[pl.ds(0, 71)], isem.at[3]),
        pltpu.make_async_copy(msk.at[0], MK, isem.at[4]),
        pltpu.make_async_copy(adj.at[0], F.at[0, :, :, pl.ds(0, 16), :], isem.at[5]),
    ]
    bar = pltpu.get_barrier_semaphore()
    lon_peers = [(mp, lat, (lon + i) & 15) for i in (8, 9, 7, 10, 6, 11, 5, 12, 4, 13, 3, 14, 2, 15, 1)]
    lat_peers = [
        (lax.rem(mp + h, 2), (x_lo ^ a) * 4 + ((y + b) & 3), lon)
        for h in (1, 0) for a in (0, 1) for b in (2, 1, 3, 0) if h or a or b
    ]
    for peer in lat_peers + lon_peers:
        pl.semaphore_signal(bar, inc=1, device_id=peer, device_id_type=MESH)
    for load in loads:
        load.start()

    lane = iota((16, 128), 1)
    row = iota((16, 128), 0)
    sub8 = iota((8, 128), 0)
    big_lane = iota((128, 128), 1)
    big_row = iota((128, 128), 0)

    KAP[71] = jnp.zeros((16, 128), F32)
    BNE[...] = jnp.zeros((128, 128), F32)

    loads[0].wait()
    p_row = jnp.broadcast_to(PT[...], (128, 128))
    t_row = p_row // 128
    diag = big_row == big_lane
    p_col = jnp.sum(jnp.where(diag, p_row.astype(F32), 0.0), axis=1, keepdims=True)
    p_col = jnp.broadcast_to(p_col, (128, 128)).astype(jnp.int32)
    t_col, l_col = p_col // 128, p_col & 127
    same = t_row == t_col
    t_send = jnp.sum(jnp.where(big_row == (big_lane ^ 7), t_col.astype(F32), 0.0), axis=0, keepdims=True)
    t_send = jnp.broadcast_to(t_send, (128, 128))
    earlier = (t_send == t_col.astype(F32)) & (big_row < (big_lane ^ 7))
    k_send = jnp.sum(jnp.where(earlier, 1.0, 0.0), axis=0, keepdims=True)
    k_send = jnp.broadcast_to(k_send, (128, 128))
    k_arr = jnp.sum(jnp.where(same & ((p_row & 127) < l_col), 1.0, 0.0), axis=1, keepdims=True)
    KM[...] = jnp.broadcast_to(k_arr, (128, 128))
    loads[1].wait()
    loads[2].wait()
    loads[3].wait()
    a1 = CP[...] * KAP[0]
    a0 = CP[...] - a1
    ST[0:16] = a0
    ST[16:32] = a1
    ST[32:40] = jnp.where(sub8 == 0, t_send[0:8], k_send[0:8])
    CF[0] = 1.0 - CO[0] - CO[1]

    pl.semaphore_wait(bar, 30)
    statics = [
        pltpu.make_async_remote_copy(
            src_ref=src, dst_ref=dst, send_sem=ts.at[i], recv_sem=tr.at[i],
            device_id=dev, device_id_type=MESH,
        )
        for i, (src, dst, dev) in enumerate((
            (ST, STW, east), (ST, STS, north), (CO.at[0], CZE, west), (CO.at[1], CMN, south),
        ))
    ]
    for copy in statics:
        copy.start()
    for peer in lat_peers:
        pl.semaphore_signal(stage, inc=1, device_id=peer, device_id_type=MESH)

    rows_f = big_row.astype(F32)
    OHP[:, 0:128] = jnp.where((t_send == rows_f) & (k_send == 0.0), 1.0, 0.0).astype(BF16)
    OHP[:, 128:256] = jnp.where((t_send == rows_f) & (k_send == 1.0), 1.0, 0.0).astype(BF16)
    LA[0:128] = jnp.where(t_col == big_lane, 1.0, 0.0).astype(BF16)
    LA[128:256] = jnp.where(((l_col // 8) == 15) & (big_lane == t_col + 16), 1.0, 0.0).astype(BF16)
    t_east = (t_col - (t_col & 15)) + ((t_col + 1) & 15)
    LB[...] = jnp.where(((l_col & 7) == 7) & (big_lane == t_east), 1.0, 0.0).astype(BF16)

    loads[4].wait()
    CF[1] = MK[...].astype(F32)
    loads[5].wait()

    def pack_level(k, edges):
        return tuple(
            jnp.where(lane == k, pltpu.roll(F[0, t, k, 0:16, :], k, 1), edges[t]) for t in range(2)
        )

    zero = jnp.zeros((16, 128), F32)
    packed = lax.fori_loop(0, 72, pack_level, (zero, zero))
    ES[0, 0] = packed[0]
    ES[0, 1] = packed[1]

    for copy in statics:
        copy.wait()
    t_s = jnp.broadcast_to(STS[32:33], (128, 128))
    k_s = jnp.broadcast_to(STS[33:34], (128, 128))
    t_n = jnp.where(big_lane < 8, pltpu.roll(t_s, 8, 1), pltpu.roll(t_s, 16, 1))
    k_n = jnp.where(big_lane < 8, pltpu.roll(k_s, 8, 1), pltpu.roll(k_s, 16, 1))
    OHX[0:128] = jnp.where(
        (big_lane < 16) & (t_n == rows_f) & (k_n == jnp.where(big_lane < 8, 0.0, 1.0)), 1.0, 0.0
    ).astype(BF16)
    pick = big_row == 8 * (big_lane & 15)
    t_wc = jnp.sum(jnp.where(diag, jnp.broadcast_to(STW[32:33], (128, 128)), 0.0), axis=1, keepdims=True)
    k_wc = jnp.sum(jnp.where(diag, jnp.broadcast_to(STW[33:34], (128, 128)), 0.0), axis=1, keepdims=True)
    t_e = jnp.sum(jnp.where(pick, jnp.broadcast_to(t_wc, (128, 128)), 0.0), axis=0, keepdims=True)
    k_e = jnp.sum(jnp.where(pick, jnp.broadcast_to(k_wc, (128, 128)), 0.0), axis=0, keepdims=True)
    OHX[128:256] = jnp.where(
        (big_lane >= 16) & (big_lane < 48)
        & (jnp.broadcast_to(t_e, (128, 128)) == rows_f)
        & (jnp.broadcast_to(k_e, (128, 128)) == jnp.where(big_lane < 32, 0.0, 1.0)),
        1.0, 0.0,
    ).astype(BF16)
    has_south = jnp.where(lat > 0, 1.0, 0.0)
    has_north = jnp.where(lat < 7, 1.0, 0.0)
    ROWS[0] = jnp.broadcast_to(STS[15:16], (8, 128)) * has_south
    ROWS[1] = jnp.broadcast_to(STS[31:32], (8, 128)) * has_south
    CF[2] = jnp.broadcast_to(STW[0:16, 127:128], (16, 128))
    CF[3] = jnp.broadcast_to(STW[16:32, 127:128], (16, 128))
    CF[4] = jnp.broadcast_to(CZE[:, 0:1], (16, 128))
    CMS[0:16] = CO[1]
    CMS[16:24] = jnp.broadcast_to(CMN[0:1], (8, 128)) * has_north
    CF[5] = CMS[1:17]

    pl.semaphore_wait(stage, 15)

    def to_tiles(ref, rows):
        parts = []
        for t in range(2):
            full = jnp.concatenate([ref[t, pl.ds(r, 8, stride=0), :] for r in range(rows)], axis=0)
            parts.append(pltpu.roll(full, 16, 1, stride=16, stride_axis=0))
        lanes = iota((8 * rows, 128), 1)
        both = jnp.where(lanes < 16, parts[0], parts[1])
        return jnp.where(lanes < 32, both, 0.0)

    def send_surface(s):
        cz, cm = CO[0], CO[1]
        weight = CF[0]
        c0, c1 = ST[0:16], ST[16:32]
        edge = jnp.zeros((16, 128), F32)
        for t in range(2):
            f0, f1 = F[s, t, 0, 0:16, :], F[s, t, 1, 0:16, :]
            z0, z1, m0, m1 = cz * f0, cz * f1, cm * f0, cm * f1
            own = jnp.zeros((16, 128), F32)
            for c, f, zf, mf in ((c0, f0, z0, m0), (c1, f1, z1, m1)):
                east_next = jnp.where(lane == 127, 0.0, pltpu.roll(zf, 127, 1))
                north_next = jnp.where(row == 15, 0.0, pltpu.roll(mf, 15, 0))
                own += c * (weight * f + east_next + north_next)
            to_south = ROWS[0] * m0[0:8] + ROWS[1] * m1[0:8]
            SURF[t] = pltpu.roll(own, 16, 1) if t else own
            NROW[t] = pltpu.roll(to_south, 16, 1) if t else to_south
            to_west = CF[2] * z0 + CF[3] * z1
            edge = jnp.where(lane == 15 + 16 * t, pltpu.roll(to_west, 15 + 16 * t, 1), edge)
        tiles = to_tiles(SURF, 16)
        high, low = halves(tiles)
        north_tiles = pltpu.roll(to_tiles(NROW, 1), 32, 1)
        BNE[0:8] = north_tiles
        BNE[8:16] = pltpu.roll(north_tiles, 64, 1)
        BNE[16:32] = edge
        BNE[32:48] = pltpu.roll(edge, 64, 1)
        first = dot(OHP[:, 0:128], jnp.concatenate([high, low], axis=1))
        second = dot(OHP[:, 128:256], jnp.concatenate([high, low], axis=1))
        extra = dot(OHX[...], jnp.concatenate(halves(BNE[...]), axis=1))
        SB[s, 0] = joined(first) + pltpu.roll(joined(second), 64, 1) + joined(extra[0:128])
        SB[s, 1] = joined(extra[128:256])
        for a, b, c, d in OFFSETS:
            to_lat = (x_lo ^ a) * 4 + ((y + b) & 3)
            to_lon = ((z + c) & 7) * 2 + (core ^ d)
            pltpu.make_async_remote_copy(
                src_ref=SB.at[s, :, pl.ds(to_lat * 16 + to_lon, 1), :],
                dst_ref=RB.at[s, :, pl.ds(me, 1), :],
                send_sem=xs.at[s], recv_sem=xr.at[s],
                device_id=(1 - mp, to_lat, to_lon), device_id_type=MESH,
            ).start()

    def edge_copies(s):
        return (
            pltpu.make_async_remote_copy(
                src_ref=F.at[s, :, :, pl.ds(0, 1), :], dst_ref=F.at[s, :, :, pl.ds(16, 1), :],
                send_sem=ns.at[s], recv_sem=nr.at[s], device_id=south, device_id_type=MESH,
            ),
            pltpu.make_async_remote_copy(
                src_ref=ES.at[s], dst_ref=EE.at[s],
                send_sem=es.at[s], recv_sem=er.at[s], device_id=west, device_id_type=MESH,
            ),
        )

    def received_surface(s):
        ga = dot(LA[...], jnp.concatenate(halves(RB[s, 0]), axis=1))
        gb = dot(LB[...], jnp.concatenate(halves(RB[s, 1]), axis=1))
        ga = joined(ga)
        x = ga[0:128] + joined(gb) + pltpu.roll(ga[128:256], 96, 1)
        tiles = jnp.where(KM[...] == 0.0, x, pltpu.roll(x, 64, 1))
        spread = pltpu.roll(tiles, 0, 1, stride=16, stride_axis=0)
        out_t = []
        for t in range(2):
            keep = (big_lane // 16) == ((big_row + t) & 7)
            out_t.append(jnp.sum(jnp.where(keep, spread, 0.0).reshape(16, 8, 128), axis=1))
        return out_t[0], pltpu.roll(out_t[1], 112, 1)

    def step(s, carry):
        send_surface(s)
        copies = edge_copies(s)
        for copy in copies:
            copy.start()
        for copy in copies:
            copy.wait()
        cz, weight, cms = CO[0], CF[0], CF[5]
        columns = [EE[s, t] * CF[4] for t in range(2)]

        def advected(t, k):
            f, f_north = F[s, t, k, 0:16, :], F[s, t, k, 1:17, :]
            column = pltpu.roll(columns[t], 127 - k, 1)
            east_next = jnp.where(lane == 127, column, pltpu.roll(cz * f, 127, 1))
            return weight * f + east_next + cms * f_north

        def level(k, state):
            kappa = KAP[k]
            after = jnp.minimum(k + 1, 71)
            new = []
            for t in range(2):
                here, flux_below, edge = state[t]
                above = advected(t, after)
                flux = kappa * (above - here)
                mixed = here + flux - flux_below
                F[s + 1, t, k, 0:16, :] = mixed
                edge = jnp.where(lane == k, pltpu.roll(mixed, k, 1), edge)
                new.append((above, flux, edge))
            return tuple(new)

        def block(b, state):
            for j in range(8):
                state = level(b * 8 + j, state)
            return state

        state = tuple((advected(t, 0), zero, zero) for t in range(2))
        state = lax.fori_loop(0, 9, block, state)

        @pl.when(s == STEPS - 1)
        def _():
            pltpu.make_async_copy(
                F.at[STEPS, :, pl.ds(1, 71), pl.ds(0, 16), :], out.at[0, :, pl.ds(1, 71)], osem.at[0]
            ).start()

        pltpu.make_async_copy(RB.at[s], RB.at[s], xr.at[s]).wait()
        received = received_surface(s)
        for t in range(2):
            mixed = F[s + 1, t, 0, 0:16, :]
            surface = mixed + CF[1] * (received[t] - CP[...] * mixed)
            F[s + 1, t, 0, 0:16, :] = surface

            @pl.when(s < STEPS - 1)
            def _():
                ES[s + 1, t] = jnp.where(lane == 0, surface, state[t][2])
        return carry

    lax.fori_loop(0, STEPS, step, 0)

    last = pltpu.make_async_copy(
        F.at[STEPS, :, pl.ds(0, 1), pl.ds(0, 16), :], out.at[0, :, pl.ds(0, 1)], osem.at[1]
    )
    last.start()
    for s in range(STEPS):
        pltpu.make_async_copy(SB.at[s], SB.at[s], xs.at[s]).wait()
    pltpu.make_async_copy(
        F.at[STEPS, :, pl.ds(1, 71), pl.ds(0, 16), :], out.at[0, :, pl.ds(1, 71)], osem.at[0]
    ).wait()
    last.wait()


def local(adjoint, courant, diffusivity, coupling, partner, mask):
    any_space = pl.BlockSpec(memory_space=pl.ANY)
    vmem = pltpu.VMEM
    dma = pltpu.SemaphoreType.DMA
    return pl.pallas_call(
        kernel,
        out_shape=jax.ShapeDtypeStruct(adjoint.shape, F32),
        in_specs=[any_space] * 6,
        out_specs=any_space,
        scratch_shapes=[
            vmem((STEPS + 1, 2, 72, 24, 128), F32),
            vmem((2, 16, 128), F32),
            vmem((72, 16, 128), F32),
            vmem((16, 128), F32),
            vmem((1, 128), jnp.int32),
            vmem((16, 128), jnp.int32),
            vmem((40, 128), F32),
            vmem((40, 128), F32),
            vmem((40, 128), F32),
            vmem((16, 128), F32),
            vmem((16, 128), F32),
            vmem((24, 128), F32),
            vmem((STEPS, 2, 16, 128), F32),
            vmem((STEPS, 2, 16, 128), F32),
            vmem((STEPS, 2, 128, 128), F32),
            vmem((STEPS, 2, 128, 128), F32),
            vmem((2, 16, 128), F32),
            vmem((2, 8, 128), F32),
            vmem((128, 128), F32),
            vmem((128, 256), BF16),
            vmem((256, 128), BF16),
            vmem((256, 128), BF16),
            vmem((128, 128), BF16),
            vmem((128, 128), F32),
            vmem((6, 16, 128), F32),
            vmem((2, 8, 128), F32),
            dma((6,)),
            dma((2,)),
            dma((STEPS,)),
            dma((STEPS,)),
            dma((STEPS,)),
            dma((STEPS,)),
            dma((STEPS,)),
            dma((STEPS,)),
            dma((4,)),
            dma((4,)),
            pltpu.SemaphoreType.REGULAR,
        ],
        compiler_params=pltpu.CompilerParams(collective_id=0, has_side_effects=True),
    )(adjoint, courant, diffusivity, coupling, partner, mask)


def solution(mesh):
    placed = (
        P("mp", None, None, "lat", "lon"),
        P("mp", None, "lat", "lon"),
        P("mp", None, "lat", "lon"),
        P("mp", "lat", "lon"),
        P("mp", ("lat", "lon")),
        P("mp", "lat", "lon"),
    )
    return jax.shard_map(
        local,
        mesh=mesh,
        in_specs=placed,
        out_specs=P("mp", None, None, "lat", "lon"),
        check_vma=False,
    )
```

```python
import functools

import jax
import jax.numpy as jnp
from jax import lax
from jax.experimental import pallas as pl
from jax.experimental.pallas import tpu as pltpu
from jax.sharding import PartitionSpec as P

TILE = 16
STEPS = 4
BLOCK = 12
MESH = pl.DeviceIdType.MESH
F32 = jnp.float32
BF16 = jnp.bfloat16


def hops(a, b, c):
    return (1 if a else 2) + min(b, 4 - b) + min(c, 8 - c)


OFFSETS = sorted(
    [(a, b, c, d) for a in range(2) for b in range(4) for c in range(8) for d in range(2)],
    key=lambda o: -hops(*o[:3]),
)


def iota(shape, axis):
    return lax.broadcasted_iota(jnp.int32, shape, axis)


def halves(x):
    high = x.astype(BF16)
    low = (x - high.astype(F32)).astype(BF16)
    return high, low


def dot(a, b):
    return jnp.dot(a, b, preferred_element_type=F32)


def joined(x):
    return x[:, :128] + x[:, 128:]


def kernel(
    adj, cour, diff, coup, part, msk, out,
    F, CO, KAP, CP, PT, MK, ST, STW, STS, CZE, CMN, CMS,
    ES, EE, SB, RB, SURF, NROW, BNE, OHP, OHX, LA, LB, KM, CF, ROWS,
    isem, osem, xs, xr, ns, nr, es, er, ts, tr, stage,
):
    mp, lat, lon = lax.axis_index("mp"), lax.axis_index("lat"), lax.axis_index("lon")
    me = lat * 16 + lon
    x_lo, y = lat // 4, lax.rem(lat, 4)
    z, core = lon // 2, lax.rem(lon, 2)
    east, west = (mp, lat, (lon + 1) & 15), (mp, lat, (lon + 15) & 15)
    north, south = (mp, (lat + 1) & 7, lon), (mp, (lat + 7) & 7, lon)

    loads = [
        pltpu.make_async_copy(part, PT, isem.at[0]),
        pltpu.make_async_copy(cour.at[0], CO, isem.at[1]),
        pltpu.make_async_copy(coup.at[0], CP, isem.at[2]),
        pltpu.make_async_copy(diff.at[0], KAP.at[pl.ds(0, 71)], isem.at[3]),
        pltpu.make_async_copy(msk.at[0], MK, isem.at[4]),
        pltpu.make_async_copy(adj.at[0], F.at[0, :, :, pl.ds(0, 16), :], isem.at[5]),
    ]
    bar = pltpu.get_barrier_semaphore()
    lon_peers = [(mp, lat, (lon + i) & 15) for i in (8, 9, 7, 10, 6, 11, 5, 12, 4, 13, 3, 14, 2, 15, 1)]
    lat_peers = [
        (lax.rem(mp + h, 2), (x_lo ^ a) * 4 + ((y + b) & 3), lon)
        for h in (1, 0) for a in (0, 1) for b in (2, 1, 3, 0) if h or a or b
    ]
    for peer in lat_peers + lon_peers:
        pl.semaphore_signal(bar, inc=1, device_id=peer, device_id_type=MESH)
    for load in loads:
        load.start()

    lane = iota((16, 128), 1)
    row = iota((16, 128), 0)
    sub8 = iota((8, 128), 0)
    big_lane = iota((128, 128), 1)
    big_row = iota((128, 128), 0)

    KAP[71] = jnp.zeros((16, 128), F32)
    BNE[...] = jnp.zeros((128, 128), F32)

    loads[0].wait()
    p_row = jnp.broadcast_to(PT[...], (128, 128))
    t_row = p_row // 128
    diag = big_row == big_lane
    p_col = jnp.sum(jnp.where(diag, p_row.astype(F32), 0.0), axis=1, keepdims=True)
    p_col = jnp.broadcast_to(p_col, (128, 128)).astype(jnp.int32)
    t_col, l_col = p_col // 128, p_col & 127
    same = t_row == t_col
    t_send = jnp.sum(jnp.where(big_row == (big_lane ^ 7), t_col.astype(F32), 0.0), axis=0, keepdims=True)
    t_send = jnp.broadcast_to(t_send, (128, 128))
    earlier = (t_send == t_col.astype(F32)) & (big_row < (big_lane ^ 7))
    k_send = jnp.sum(jnp.where(earlier, 1.0, 0.0), axis=0, keepdims=True)
    k_send = jnp.broadcast_to(k_send, (128, 128))
    k_arr = jnp.sum(jnp.where(same & ((p_row & 127) < l_col), 1.0, 0.0), axis=1, keepdims=True)
    KM[...] = jnp.broadcast_to(k_arr, (128, 128))
    loads[1].wait()
    loads[2].wait()
    loads[3].wait()
    a1 = CP[...] * KAP[0]
    a0 = CP[...] - a1
    ST[0:16] = a0
    ST[16:32] = a1
    ST[32:40] = jnp.where(sub8 == 0, t_send[0:8], k_send[0:8])
    CF[0] = 1.0 - CO[0] - CO[1]

    pl.semaphore_wait(bar, 30)
    statics = [
        pltpu.make_async_remote_copy(
            src_ref=src, dst_ref=dst, send_sem=ts.at[i], recv_sem=tr.at[i],
            device_id=dev, device_id_type=MESH,
        )
        for i, (src, dst, dev) in enumerate((
            (ST, STW, east), (ST, STS, north), (CO.at[0], CZE, west), (CO.at[1], CMN, south),
        ))
    ]
    for copy in statics:
        copy.start()
    for peer in lat_peers:
        pl.semaphore_signal(stage, inc=1, device_id=peer, device_id_type=MESH)

    rows_f = big_row.astype(F32)
    OHP[:, 0:128] = jnp.where((t_send == rows_f) & (k_send == 0.0), 1.0, 0.0).astype(BF16)
    OHP[:, 128:256] = jnp.where((t_send == rows_f) & (k_send == 1.0), 1.0, 0.0).astype(BF16)
    LA[0:128] = jnp.where(t_col == big_lane, 1.0, 0.0).astype(BF16)
    LA[128:256] = jnp.where(((l_col // 8) == 15) & (big_lane == t_col + 16), 1.0, 0.0).astype(BF16)
    t_east = (t_col - (t_col & 15)) + ((t_col + 1) & 15)
    LB[...] = jnp.where(((l_col & 7) == 7) & (big_lane == t_east), 1.0, 0.0).astype(BF16)

    loads[4].wait()
    CF[1] = MK[...].astype(F32)
    loads[5].wait()

    def pack_level(k, edges):
        return tuple(
            jnp.where(lane == k, pltpu.roll(F[0, t, k, 0:16, :], k, 1), edges[t]) for t in range(2)
        )

    zero = jnp.zeros((16, 128), F32)
    packed = lax.fori_loop(0, 72, pack_level, (zero, zero))
    ES[0, 0] = packed[0]
    ES[0, 1] = packed[1]

    for copy in statics:
        copy.wait()
    t_s = jnp.broadcast_to(STS[32:33], (128, 128))
    k_s = jnp.broadcast_to(STS[33:34], (128, 128))
    t_n = jnp.where(big_lane < 8, pltpu.roll(t_s, 8, 1), pltpu.roll(t_s, 16, 1))
    k_n = jnp.where(big_lane < 8, pltpu.roll(k_s, 8, 1), pltpu.roll(k_s, 16, 1))
    OHX[0:128] = jnp.where(
        (big_lane < 16) & (t_n == rows_f) & (k_n == jnp.where(big_lane < 8, 0.0, 1.0)), 1.0, 0.0
    ).astype(BF16)
    pick = big_row == 8 * (big_lane & 15)
    t_wc = jnp.sum(jnp.where(diag, jnp.broadcast_to(STW[32:33], (128, 128)), 0.0), axis=1, keepdims=True)
    k_wc = jnp.sum(jnp.where(diag, jnp.broadcast_to(STW[33:34], (128, 128)), 0.0), axis=1, keepdims=True)
    t_e = jnp.sum(jnp.where(pick, jnp.broadcast_to(t_wc, (128, 128)), 0.0), axis=0, keepdims=True)
    k_e = jnp.sum(jnp.where(pick, jnp.broadcast_to(k_wc, (128, 128)), 0.0), axis=0, keepdims=True)
    OHX[128:256] = jnp.where(
        (big_lane >= 16) & (big_lane < 48)
        & (jnp.broadcast_to(t_e, (128, 128)) == rows_f)
        & (jnp.broadcast_to(k_e, (128, 128)) == jnp.where(big_lane < 32, 0.0, 1.0)),
        1.0, 0.0,
    ).astype(BF16)
    has_south = jnp.where(lat > 0, 1.0, 0.0)
    has_north = jnp.where(lat < 7, 1.0, 0.0)
    ROWS[0] = jnp.broadcast_to(STS[15:16], (8, 128)) * has_south
    ROWS[1] = jnp.broadcast_to(STS[31:32], (8, 128)) * has_south
    CF[2] = jnp.broadcast_to(STW[0:16, 127:128], (16, 128))
    CF[3] = jnp.broadcast_to(STW[16:32, 127:128], (16, 128))
    CF[4] = jnp.broadcast_to(CZE[:, 0:1], (16, 128))
    CMS[0:16] = CO[1]
    CMS[16:24] = jnp.broadcast_to(CMN[0:1], (8, 128)) * has_north
    CF[5] = CMS[1:17]

    pl.semaphore_wait(stage, 15)

    def to_tiles(ref, rows):
        parts = []
        for t in range(2):
            full = jnp.concatenate([ref[t, pl.ds(r, 8, stride=0), :] for r in range(rows)], axis=0)
            parts.append(pltpu.roll(full, 16, 1, stride=16, stride_axis=0))
        lanes = iota((8 * rows, 128), 1)
        both = jnp.where(lanes < 16, parts[0], parts[1])
        return jnp.where(lanes < 32, both, 0.0)

    def send_surface(s):
        cz, cm = CO[0], CO[1]
        weight = CF[0]
        c0, c1 = ST[0:16], ST[16:32]
        edge = jnp.zeros((16, 128), F32)
        for t in range(2):
            f0, f1 = F[s, t, 0, 0:16, :], F[s, t, 1, 0:16, :]
            z0, z1, m0, m1 = cz * f0, cz * f1, cm * f0, cm * f1
            own = jnp.zeros((16, 128), F32)
            for c, f, zf, mf in ((c0, f0, z0, m0), (c1, f1, z1, m1)):
                east_next = jnp.where(lane == 127, 0.0, pltpu.roll(zf, 127, 1))
                north_next = jnp.where(row == 15, 0.0, pltpu.roll(mf, 15, 0))
                own += c * (weight * f + east_next + north_next)
            to_south = ROWS[0] * m0[0:8] + ROWS[1] * m1[0:8]
            SURF[t] = pltpu.roll(own, 16, 1) if t else own
            NROW[t] = pltpu.roll(to_south, 16, 1) if t else to_south
            to_west = CF[2] * z0 + CF[3] * z1
            edge = jnp.where(lane == 15 + 16 * t, pltpu.roll(to_west, 15 + 16 * t, 1), edge)
        tiles = to_tiles(SURF, 16)
        high, low = halves(tiles)
        north_tiles = pltpu.roll(to_tiles(NROW, 1), 32, 1)
        BNE[0:8] = north_tiles
        BNE[8:16] = pltpu.roll(north_tiles, 64, 1)
        BNE[16:32] = edge
        BNE[32:48] = pltpu.roll(edge, 64, 1)
        first = dot(OHP[:, 0:128], jnp.concatenate([high, low], axis=1))
        second = dot(OHP[:, 128:256], jnp.concatenate([high, low], axis=1))
        extra = dot(OHX[...], jnp.concatenate(halves(BNE[...]), axis=1))
        SB[s, 0] = joined(first) + pltpu.roll(joined(second), 64, 1) + joined(extra[0:128])
        SB[s, 1] = joined(extra[128:256])
        for a, b, c, d in OFFSETS:
            to_lat = (x_lo ^ a) * 4 + ((y + b) & 3)
            to_lon = ((z + c) & 7) * 2 + (core ^ d)
            pltpu.make_async_remote_copy(
                src_ref=SB.at[s, :, pl.ds(to_lat * 16 + to_lon, 1), :],
                dst_ref=RB.at[s, :, pl.ds(me, 1), :],
                send_sem=xs.at[s], recv_sem=xr.at[s],
                device_id=(1 - mp, to_lat, to_lon), device_id_type=MESH,
            ).start()

    def edge_copies(s):
        return (
            pltpu.make_async_remote_copy(
                src_ref=F.at[s, :, :, pl.ds(0, 1), :], dst_ref=F.at[s, :, :, pl.ds(16, 1), :],
                send_sem=ns.at[s], recv_sem=nr.at[s], device_id=south, device_id_type=MESH,
            ),
            pltpu.make_async_remote_copy(
                src_ref=ES.at[s], dst_ref=EE.at[s],
                send_sem=es.at[s], recv_sem=er.at[s], device_id=west, device_id_type=MESH,
            ),
        )

    def received_surface(s):
        ga = dot(LA[...], jnp.concatenate(halves(RB[s, 0]), axis=1))
        gb = dot(LB[...], jnp.concatenate(halves(RB[s, 1]), axis=1))
        ga = joined(ga)
        x = ga[0:128] + joined(gb) + pltpu.roll(ga[128:256], 96, 1)
        tiles = jnp.where(KM[...] == 0.0, x, pltpu.roll(x, 64, 1))
        spread = pltpu.roll(tiles, 0, 1, stride=16, stride_axis=0)
        out_t = []
        for t in range(2):
            keep = (big_lane // 16) == ((big_row + t) & 7)
            out_t.append(jnp.sum(jnp.where(keep, spread, 0.0).reshape(16, 8, 128), axis=1))
        return out_t[0], pltpu.roll(out_t[1], 112, 1)

    def step(s, carry):
        send_surface(s)
        copies = edge_copies(s)
        for copy in copies:
            copy.start()
        for copy in copies:
            copy.wait()
        cz, weight, cms = CO[0], CF[0], CF[5]
        columns = [EE[s, t] * CF[4] for t in range(2)]

        def advected(t, k):
            f, f_north = F[s, t, k, 0:16, :], F[s, t, k, 1:17, :]
            column = pltpu.roll(columns[t], 127 - k, 1)
            east_next = jnp.where(lane == 127, column, pltpu.roll(cz * f, 127, 1))
            return weight * f + east_next + cms * f_north

        def block(b, state):
            first = b * BLOCK
            kappas = [KAP[first + j] for j in range(BLOCK)]
            above = [
                [advected(t, jnp.minimum(first + j + 1, 71)) for j in range(BLOCK)]
                for t in range(2)
            ]
            new = []
            for t in range(2):
                here, flux_below, edge = state[t]
                for j in range(BLOCK):
                    flux = kappas[j] * (above[t][j] - here)
                    mixed = here + flux - flux_below
                    F[s + 1, t, first + j, 0:16, :] = mixed
                    edge = jnp.where(lane == first + j, pltpu.roll(mixed, first + j, 1), edge)
                    here, flux_below = above[t][j], flux
                new.append((here, flux_below, edge))
            return tuple(new)

        state = tuple((advected(t, 0), zero, zero) for t in range(2))
        state = lax.fori_loop(0, 72 // BLOCK, block, state)

        @pl.when(s == STEPS - 1)
        def _():
            pltpu.make_async_copy(
                F.at[STEPS, :, pl.ds(1, 71), pl.ds(0, 16), :], out.at[0, :, pl.ds(1, 71)], osem.at[0]
            ).start()

        pltpu.make_async_copy(RB.at[s], RB.at[s], xr.at[s]).wait()
        received = received_surface(s)
        for t in range(2):
            mixed = F[s + 1, t, 0, 0:16, :]
            surface = mixed + CF[1] * (received[t] - CP[...] * mixed)
            F[s + 1, t, 0, 0:16, :] = surface

            @pl.when(s == STEPS - 1)
            def _():
                out[0, t, 0] = surface

            @pl.when(s < STEPS - 1)
            def _():
                ES[s + 1, t] = jnp.where(lane == 0, surface, state[t][2])
        return carry

    lax.fori_loop(0, STEPS, step, 0)

    for s in range(STEPS):
        pltpu.make_async_copy(SB.at[s], SB.at[s], xs.at[s]).wait()
    pltpu.make_async_copy(
        F.at[STEPS, :, pl.ds(1, 71), pl.ds(0, 16), :], out.at[0, :, pl.ds(1, 71)], osem.at[0]
    ).wait()


def local(adjoint, courant, diffusivity, coupling, partner, mask):
    any_space = pl.BlockSpec(memory_space=pl.ANY)
    vmem = pltpu.VMEM
    dma = pltpu.SemaphoreType.DMA
    return pl.pallas_call(
        kernel,
        out_shape=vmem(adjoint.shape, F32),
        in_specs=[any_space] * 6,
        out_specs=pl.BlockSpec(memory_space=vmem),
        scratch_shapes=[
            vmem((STEPS + 1, 2, 72, 24, 128), F32),
            vmem((2, 16, 128), F32),
            vmem((72, 16, 128), F32),
            vmem((16, 128), F32),
            vmem((1, 128), jnp.int32),
            vmem((16, 128), jnp.int32),
            vmem((40, 128), F32),
            vmem((40, 128), F32),
            vmem((40, 128), F32),
            vmem((16, 128), F32),
            vmem((16, 128), F32),
            vmem((24, 128), F32),
            vmem((STEPS, 2, 16, 128), F32),
            vmem((STEPS, 2, 16, 128), F32),
            vmem((STEPS, 2, 128, 128), F32),
            vmem((STEPS, 2, 128, 128), F32),
            vmem((2, 16, 128), F32),
            vmem((2, 8, 128), F32),
            vmem((128, 128), F32),
            vmem((128, 256), BF16),
            vmem((256, 128), BF16),
            vmem((256, 128), BF16),
            vmem((128, 128), BF16),
            vmem((128, 128), F32),
            vmem((6, 16, 128), F32),
            vmem((2, 8, 128), F32),
            dma((6,)),
            dma((1,)),
            dma((STEPS,)),
            dma((STEPS,)),
            dma((STEPS,)),
            dma((STEPS,)),
            dma((STEPS,)),
            dma((STEPS,)),
            dma((4,)),
            dma((4,)),
            pltpu.SemaphoreType.REGULAR,
        ],
        compiler_params=pltpu.CompilerParams(collective_id=0, has_side_effects=True),
    )(adjoint, courant, diffusivity, coupling, partner, mask)


def solution(mesh):
    placed = (
        P("mp", None, None, "lat", "lon"),
        P("mp", None, "lat", "lon"),
        P("mp", None, "lat", "lon"),
        P("mp", "lat", "lon"),
        P("mp", ("lat", "lon")),
        P("mp", "lat", "lon"),
    )
    return jax.shard_map(
        local,
        mesh=mesh,
        in_specs=placed,
        out_specs=P("mp", None, None, "lat", "lon"),
        check_vma=False,
    )
```

```python
import functools

import jax
import jax.numpy as jnp
from jax import lax
from jax.experimental import pallas as pl
from jax.experimental.pallas import tpu as pltpu
from jax.sharding import PartitionSpec as P

TILE = 16
STEPS = 4
BLOCK = 12
MESH = pl.DeviceIdType.MESH
F32 = jnp.float32
BF16 = jnp.bfloat16


def hops(a, b, c):
    return (1 if a else 2) + min(b, 4 - b) + min(c, 8 - c)


OFFSETS = sorted(
    [(a, b, c, d) for a in range(2) for b in range(4) for c in range(8) for d in range(2)],
    key=lambda o: -hops(*o[:3]),
)


def iota(shape, axis):
    return lax.broadcasted_iota(jnp.int32, shape, axis)


def halves(x):
    high = x.astype(BF16)
    low = (x - high.astype(F32)).astype(BF16)
    return high, low


def dot(a, b):
    return jnp.dot(a, b, preferred_element_type=F32)


def kernel(
    adj, cour, diff, coup, part, msk, out,
    F, CO, KAP, CP, PT, MK, ST, STW, STS, CZE, CMN, CMS,
    ES, EE, E01, E01N, SB, RB, OHP, OHX, LR, KM, CF, ROWS, ZP,
    isem, osem, xs, xr, ns, nr, es, er, ts, tr, stage,
):
    mp, lat, lon = lax.axis_index("mp"), lax.axis_index("lat"), lax.axis_index("lon")
    me = lat * 16 + lon
    x_lo, y = lat // 4, lax.rem(lat, 4)
    z, core = lon // 2, lax.rem(lon, 2)
    east, west = (mp, lat, (lon + 1) & 15), (mp, lat, (lon + 15) & 15)
    north, south = (mp, (lat + 1) & 7, lon), (mp, (lat + 7) & 7, lon)

    loads = [
        pltpu.make_async_copy(src, dst, isem.at[i])
        for i, (src, dst) in enumerate((
            (adj.at[0, :, pl.ds(0, 2)], F.at[0, :, pl.ds(0, 2), pl.ds(0, 16), :]),
            (cour.at[0], CO),
            (part, PT),
            (diff.at[0, pl.ds(0, 1)], KAP.at[pl.ds(0, 1)]),
            (coup.at[0], CP),
            (msk.at[0], MK),
            (diff.at[0, pl.ds(1, 70)], KAP.at[pl.ds(1, 70)]),
            (adj.at[0, :, pl.ds(2, 70)], F.at[0, :, pl.ds(2, 70), pl.ds(0, 16), :]),
        ))
    ]
    bar = pltpu.get_barrier_semaphore()
    lon_peers = [(mp, lat, (lon + i) & 15) for i in (8, 9, 7, 10, 6, 11, 5, 12, 4, 13, 3, 14, 2, 15, 1)]
    lat_peers = [
        (lax.rem(mp + h, 2), (x_lo ^ a) * 4 + ((y + b) & 3), lon)
        for h in (1, 0) for a in (0, 1) for b in (2, 1, 3, 0) if h or a or b
    ]
    for peer in lat_peers + lon_peers:
        pl.semaphore_signal(bar, inc=1, device_id=peer, device_id_type=MESH)
    for load in loads:
        load.start()

    lane = iota((16, 128), 1)
    row = iota((16, 128), 0)
    sub8 = iota((8, 128), 0)
    big_lane = iota((128, 128), 1)
    big_row = iota((128, 128), 0)

    KAP[71] = jnp.zeros((16, 128), F32)
    ZP[...] = jnp.zeros((128, 128), F32)

    perm_lane = (big_lane & 15) * 8 + big_lane // 16
    perm_row = (big_row & 15) * 8 + big_row // 16
    rows_f = big_row.astype(F32)
    lanes_f = big_lane.astype(F32)

    def total(mask, values, axis):
        kept = jnp.sum(jnp.where(mask, values, 0.0), axis=axis, keepdims=True)
        return jnp.broadcast_to(kept, (128, 128))

    def remote(src, dst, send, recv, dev):
        return pltpu.make_async_remote_copy(
            src_ref=src, dst_ref=dst, send_sem=send, recv_sem=recv,
            device_id=dev, device_id_type=MESH,
        )

    def edge_copies(s):
        return (
            remote(
                F.at[s, :, :, pl.ds(0, 1), :], F.at[s, :, :, pl.ds(16, 1), :],
                ns.at[s], nr.at[s], south,
            ),
            remote(ES.at[s], EE.at[s], es.at[s], er.at[s], west),
        )

    zero = jnp.zeros((16, 128), F32)
    loads[0].wait()
    for t in range(2):
        E01[t] = jnp.where(lane == 0, F[0, t, 0, 0:16, :], pltpu.roll(F[0, t, 1, 0:16, :], 1, 1))
    loads[1].wait()
    pl.semaphore_wait(bar, 30)
    early = [
        remote(src, dst, ts.at[i], tr.at[i], dev)
        for i, (src, dst, dev) in enumerate((
            (E01, E01N, west),
            (F.at[0, :, pl.ds(0, 2), pl.ds(0, 1), :], F.at[0, :, pl.ds(0, 2), pl.ds(16, 1), :], south),
            (CO.at[0], CZE, west),
            (CO.at[1, pl.ds(0, 8)], CMN, south),
        ))
    ]
    for peer in lat_peers:
        pl.semaphore_signal(stage, inc=1, device_id=peer, device_id_type=MESH)
    for copy in early:
        copy.start()

    loads[2].wait()
    p_row = jnp.broadcast_to(PT[...], (128, 128))
    t_row, l_row = (p_row // 128).astype(F32), (p_row & 127).astype(F32)
    t_col = total(big_row == big_lane, t_row, 1)

    def sent(order):
        target = total(big_row == order, t_col, 0)
        slot = total((t_col == target) & (big_row < order), 1.0, 0)
        return target, slot

    t_send, k_send = sent(perm_lane)
    t_rev, k_rev = sent(big_lane ^ 7)
    t_from = total(big_lane == perm_row, t_row, 1)
    l_from = total(big_lane == perm_row, l_row, 1)
    KM[...] = total((t_row == t_from) & (l_row < l_from), 1.0, 1)
    loads[3].wait()
    loads[4].wait()
    a1 = CP[...] * KAP[0]
    a0 = CP[...] - a1
    ST[0:16] = a0
    ST[16:32] = a1
    ST[32:40] = jnp.where(
        sub8 == 0, t_send[0:8],
        jnp.where(sub8 == 1, k_send[0:8], jnp.where(sub8 == 2, t_rev[0:8], k_rev[0:8])),
    )
    CF[0] = 1.0 - CO[0] - CO[1]
    for half in (0, 256):
        for k in (0, 1):
            OHP[:, half + 128 * k:half + 128 * k + 128] = jnp.where(
                (t_send == rows_f) & (k_send == float(k)), 1.0, 0.0
            ).astype(BF16)
    for load in loads[5:]:
        load.wait()
    CF[1] = MK[...].astype(F32)

    def pack_level(k, edges):
        return tuple(
            jnp.where(lane == k, pltpu.roll(F[0, t, k, 0:16, :], k, 1), edges[t]) for t in range(2)
        )

    packed = lax.fori_loop(0, 72, pack_level, (zero, zero))
    ES[0, 0] = packed[0]
    ES[0, 1] = packed[1]

    later = [
        remote(src, dst, ts.at[4 + i], tr.at[4 + i], dev)
        for i, (src, dst, dev) in enumerate((
            (ES.at[0], EE.at[0], west),
            (F.at[0, :, pl.ds(2, 70), pl.ds(0, 1), :], F.at[0, :, pl.ds(2, 70), pl.ds(16, 1), :], south),
            (ST, STW, east),
            (ST, STS, north),
        ))
    ]
    for copy in later:
        copy.start()
    for copy in early:
        copy.wait()
    has_north = jnp.where(lat < 7, 1.0, 0.0)
    CF[4] = jnp.broadcast_to(CZE[:, 0:1], (16, 128))
    CMS[0:16] = CO[1]
    CMS[16:24] = jnp.broadcast_to(CMN[0:1], (8, 128)) * has_north
    CF[5] = CMS[1:17]

    def edge_columns(ref):
        return [ref[t] * CF[4] for t in range(2)]

    def advected(s, t, k, columns):
        f, f_north = F[s, t, k, 0:16, :], F[s, t, k, 1:17, :]
        column = pltpu.roll(columns[t], 127 - k, 1)
        east_next = jnp.where(lane == 127, column, pltpu.roll(CO[0] * f, 127, 1))
        return CF[0] * f + east_next + CF[5] * f_north

    def split_rows(parts):
        pairs = [halves(part) for part in parts]
        return [pair[0] for pair in pairs] + [pair[1] for pair in pairs]

    def tile_rows(own):
        parts = []
        for c in range(8):
            first = pltpu.roll(own[0], (128 - 16 * c) & 127, 1)
            second = pltpu.roll(own[1], (144 - 16 * c) & 127, 1)
            parts.append(jnp.where(lane < 16, first, jnp.where(lane < 32, second, 0.0)))
        tiles = jnp.concatenate(parts, axis=0)
        return jnp.concatenate(split_rows([tiles, pltpu.roll(tiles, 64, 1)]), axis=0)

    def pack_first():
        columns = edge_columns(E01N)
        own = []
        for t in range(2):
            own.append(ST[0:16] * advected(0, t, 0, columns) + ST[16:32] * advected(0, t, 1, columns))
        SB[0, 0] = dot(OHP[...], tile_rows(own))

    def pack(s, surfaces):
        cz, cm = CO[0], CO[1]
        edge = jnp.zeros((16, 128), F32)
        own, north_parts = [], []
        for t in range(2):
            f0, f1 = surfaces[t], F[s, t, 1, 0:16, :]
            z0, z1, m0, m1 = cz * f0, cz * f1, cm * f0, cm * f1
            value = jnp.zeros((16, 128), F32)
            for c, f, zf, mf in ((ST[0:16], f0, z0, m0), (ST[16:32], f1, z1, m1)):
                east_next = jnp.where(lane == 127, 0.0, pltpu.roll(zf, 127, 1))
                north_next = jnp.where(row == 15, 0.0, pltpu.roll(mf, 15, 0))
                value += c * (CF[0] * f + east_next + north_next)
            own.append(value)
            to_south = jnp.broadcast_to((ROWS[0] * m0[0:8] + ROWS[1] * m1[0:8])[0:1], (8, 128))
            if t:
                to_south = pltpu.roll(to_south, 16, 1)
            north_parts.append(pltpu.roll(to_south, 16, 1, stride=16, stride_axis=0))
            to_west = CF[2] * z0 + CF[3] * z1
            edge = jnp.where(lane == 15 + 16 * t, pltpu.roll(to_west, 15 + 16 * t, 1), edge)
        lanes = iota((8, 128), 1)
        both = jnp.where(lanes < 16, north_parts[0], jnp.where(lanes < 32, north_parts[1], 0.0))
        north_tiles = pltpu.roll(both, 32, 1)
        added = jnp.concatenate(
            [north_tiles, pltpu.roll(north_tiles, 64, 1), edge, pltpu.roll(edge, 64, 1), zero], axis=0
        )
        extra = jnp.concatenate(split_rows([added]), axis=0)
        SB[s, 0] = dot(OHP[...], tile_rows(own)) + dot(OHX[0:128], extra)
        SB[s, 1] = dot(OHX[128:256], extra)

    def send(s, count):
        planes = pl.ds(0, count)
        for a, b, c, d in OFFSETS:
            to_lat = (x_lo ^ a) * 4 + ((y + b) & 3)
            to_lon = ((z + c) & 7) * 2 + (core ^ d)
            remote(
                SB.at[s, planes, pl.ds(to_lat * 16 + to_lon, 1), :],
                RB.at[s, planes, pl.ds(me, 1), :],
                xs.at[s], xr.at[s], (1 - mp, to_lat, to_lon),
            ).start()

    def deep_copy():
        return pltpu.make_async_copy(
            F.at[STEPS, :, pl.ds(1, 71), pl.ds(0, 16), :], out.at[0, :, pl.ds(1, 71)], osem.at[0]
        )

    def received_surface(s):
        plane = RB[s, 0]
        parts = [plane, pltpu.roll(plane, 96, 1), RB[s, 1]]
        gathered = dot(LR[...], jnp.concatenate([half for part in parts for half in halves(part)], axis=0))
        tiles = jnp.where(KM[...] == 0.0, gathered, pltpu.roll(gathered, 64, 1))
        out_0, out_1 = zero, zero
        for c in range(8):
            moved = pltpu.roll(tiles[16 * c:16 * c + 16], 16 * c, 1)
            out_0 = jnp.where(lane // 16 == c, moved, out_0)
            out_1 = jnp.where(lane // 16 == (c + 1) % 8, moved, out_1)
        return out_0, pltpu.roll(out_1, 112, 1)

    pack_first()
    blank = pltpu.make_async_copy(ZP, RB.at[0, 1], xr.at[0])
    blank.start()
    pl.semaphore_wait(stage, 15)
    send(0, 1)
    own_rows = (t_from == lanes_f)
    north_rows = (l_from >= 120.0) & (lanes_f == t_from + 16.0)
    t_int = t_from.astype(jnp.int32)
    t_east = (t_int - (t_int & 15)) + ((t_int + 1) & 15)
    east_rows = ((l_from.astype(jnp.int32) & 7) == 7) & (big_lane == t_east)
    for i, rows in enumerate((own_rows, own_rows, north_rows, north_rows, east_rows, east_rows)):
        LR[:, 128 * i:128 * i + 128] = jnp.where(rows, 1.0, 0.0).astype(BF16)

    for copy in later:
        copy.wait()
    spread = lambda x: jnp.broadcast_to(x, (128, 128))

    def shifted_slots(ref, first, shifts, start, count):
        t_all, k_all = spread(ref[first:first + 1]), spread(ref[first + 1:first + 2])
        hit = jnp.zeros((128, 128), F32)
        for k in (0, 1):
            for half in (0, 64):
                shift = (shifts[k] + half) & 127
                inside = (big_lane >= start + count * k + half) & (big_lane < start + count * (k + 1) + half)
                found = (pltpu.roll(t_all, shift, 1) == rows_f) & (pltpu.roll(k_all, shift, 1) == float(k))
                hit = jnp.where(inside & found, 1.0, hit)
        return hit.astype(BF16)

    OHX[0:128] = shifted_slots(STS, 34, (8, 16), 0, 8)
    OHX[128:256] = shifted_slots(STW, 32, (32, 48), 16, 16)
    has_south = jnp.where(lat > 0, 1.0, 0.0)
    ROWS[0] = jnp.broadcast_to(STS[15:16], (8, 128)) * has_south
    ROWS[1] = jnp.broadcast_to(STS[31:32], (8, 128)) * has_south
    CF[2] = jnp.broadcast_to(STW[0:16, 127:128], (16, 128))
    CF[3] = jnp.broadcast_to(STW[16:32, 127:128], (16, 128))

    def step(s, carry):
        columns = edge_columns(EE.at[s])

        def block(b, state):
            first = b * BLOCK
            above = [
                [advected(s, t, jnp.minimum(first + j + 1, 71), columns) for j in range(BLOCK)]
                for t in range(2)
            ]
            new = []
            for t in range(2):
                here, flux_below, edge = state[t]
                for j in range(BLOCK):
                    flux = KAP[first + j] * (above[t][j] - here)
                    mixed = here + flux - flux_below
                    F[s + 1, t, first + j, 0:16, :] = mixed
                    edge = jnp.where(lane == first + j, pltpu.roll(mixed, first + j, 1), edge)
                    here, flux_below = above[t][j], flux
                new.append((here, flux_below, edge))
            return tuple(new)

        state = tuple((advected(s, t, 0, columns), zero, zero) for t in range(2))
        state = lax.fori_loop(0, 72 // BLOCK, block, state)

        @pl.when(s == STEPS - 1)
        def _():
            deep_copy().start()

        pltpu.make_async_copy(RB.at[s], RB.at[s], xr.at[s]).wait()
        received = received_surface(s)
        surfaces = []
        for t in range(2):
            mixed = F[s + 1, t, 0, 0:16, :]
            surfaces.append(mixed + CF[1] * (received[t] - CP[...] * mixed))

        @pl.when(s < STEPS - 1)
        def _():
            for t in range(2):
                F[s + 1, t, 0, 0:16, :] = surfaces[t]
                ES[s + 1, t] = jnp.where(lane == 0, surfaces[t], state[t][2])
            copies = edge_copies(s + 1)
            for copy in copies:
                copy.start()
            pack(s + 1, surfaces)
            send(s + 1, 2)
            for copy in copies:
                copy.wait()

        @pl.when(s == STEPS - 1)
        def _():
            for t in range(2):
                out[0, t, 0] = surfaces[t]

        return carry

    lax.fori_loop(0, STEPS, step, 0)
    for s in range(STEPS):
        gone = SB.at[s] if s else SB.at[s, 0]
        pltpu.make_async_copy(gone, gone, xs.at[s]).wait()
    deep_copy().wait()


def local(adjoint, courant, diffusivity, coupling, partner, mask):
    any_space = pl.BlockSpec(memory_space=pl.ANY)
    vmem = pltpu.VMEM
    dma = pltpu.SemaphoreType.DMA
    return pl.pallas_call(
        kernel,
        out_shape=vmem(adjoint.shape, F32),
        in_specs=[any_space] * 6,
        out_specs=pl.BlockSpec(memory_space=vmem),
        scratch_shapes=[
            vmem((STEPS + 1, 2, 72, 24, 128), F32),
            vmem((2, 16, 128), F32),
            vmem((72, 16, 128), F32),
            vmem((16, 128), F32),
            vmem((1, 128), jnp.int32),
            vmem((16, 128), jnp.int32),
            vmem((40, 128), F32),
            vmem((40, 128), F32),
            vmem((40, 128), F32),
            vmem((16, 128), F32),
            vmem((8, 128), F32),
            vmem((24, 128), F32),
            vmem((STEPS, 2, 16, 128), F32),
            vmem((STEPS, 2, 16, 128), F32),
            vmem((2, 16, 128), F32),
            vmem((2, 16, 128), F32),
            vmem((STEPS, 2, 128, 128), F32),
            vmem((STEPS, 2, 128, 128), F32),
            vmem((128, 512), BF16),
            vmem((256, 128), BF16),
            vmem((128, 768), BF16),
            vmem((128, 128), F32),
            vmem((6, 16, 128), F32),
            vmem((2, 8, 128), F32),
            vmem((128, 128), F32),
            dma((8,)),
            dma((1,)),
            dma((STEPS,)),
            dma((STEPS,)),
            dma((STEPS,)),
            dma((STEPS,)),
            dma((STEPS,)),
            dma((STEPS,)),
            dma((8,)),
            dma((8,)),
            pltpu.SemaphoreType.REGULAR,
        ],
        compiler_params=pltpu.CompilerParams(collective_id=0, has_side_effects=True),
    )(adjoint, courant, diffusivity, coupling, partner, mask)


def solution(mesh):
    placed = (
        P("mp", None, None, "lat", "lon"),
        P("mp", None, "lat", "lon"),
        P("mp", None, "lat", "lon"),
        P("mp", "lat", "lon"),
        P("mp", ("lat", "lon")),
        P("mp", "lat", "lon"),
    )
    return jax.shard_map(
        local,
        mesh=mesh,
        in_specs=placed,
        out_specs=P("mp", None, None, "lat", "lon"),
        check_vma=False,
    )
```

```python
import functools

import jax
import jax.numpy as jnp
from jax import lax
from jax.experimental import pallas as pl
from jax.experimental.pallas import tpu as pltpu
from jax.sharding import PartitionSpec as P

TILE = 16
STEPS = 4
BLOCK = 12
MESH = pl.DeviceIdType.MESH
F32 = jnp.float32
BF16 = jnp.bfloat16


def hops(a, b, c):
    return (1 if a else 2) + min(b, 4 - b) + min(c, 8 - c)


OFFSETS = sorted(
    [(a, b, c, d) for a in range(2) for b in range(4) for c in range(8) for d in range(2)],
    key=lambda o: -(hops(o[0], o[1], 0) + 1.6 * min(o[2], 8 - o[2])),
)


def iota(shape, axis):
    return lax.broadcasted_iota(jnp.int32, shape, axis)


def halves(x):
    high = x.astype(BF16)
    low = (x - high.astype(F32)).astype(BF16)
    return high, low


def dot(a, b):
    return jnp.dot(a, b, preferred_element_type=F32)


def kernel(
    adj, cour, diff, coup, part, msk, out,
    F, CO, KAP, CP, PT, MK, ST, STW, STS, CZE, CMN, CMS,
    ES, EE, E01, E01N, SB, RB, OHP, OHX, LR, KM, CF, ROWS, ZP,
    isem, osem, xs, xr, ns, nr, es, er, ts, tr, stage,
):
    mp, lat, lon = lax.axis_index("mp"), lax.axis_index("lat"), lax.axis_index("lon")
    me = lat * 16 + lon
    x_lo, y = lat // 4, lax.rem(lat, 4)
    z, core = lon // 2, lax.rem(lon, 2)
    east, west = (mp, lat, (lon + 1) & 15), (mp, lat, (lon + 15) & 15)
    north, south = (mp, (lat + 1) & 7, lon), (mp, (lat + 7) & 7, lon)

    loads = [
        pltpu.make_async_copy(src, dst, isem.at[i])
        for i, (src, dst) in enumerate((
            (adj.at[0, :, pl.ds(0, 2)], F.at[0, :, pl.ds(0, 2), pl.ds(0, 16), :]),
            (cour.at[0], CO),
            (part, PT),
            (diff.at[0, pl.ds(0, 1)], KAP.at[pl.ds(0, 1)]),
            (coup.at[0], CP),
            (msk.at[0], MK),
            (diff.at[0, pl.ds(1, 70)], KAP.at[pl.ds(1, 70)]),
            (adj.at[0, :, pl.ds(2, 70)], F.at[0, :, pl.ds(2, 70), pl.ds(0, 16), :]),
        ))
    ]
    bar = pltpu.get_barrier_semaphore()
    lon_peers = [(mp, lat, (lon + i) & 15) for i in (8, 9, 7, 10, 6, 11, 5, 12, 4, 13, 3, 14, 2, 15, 1)]
    lat_peers = [
        (lax.rem(mp + h, 2), (x_lo ^ a) * 4 + ((y + b) & 3), lon)
        for h in (1, 0) for a in (0, 1) for b in (2, 1, 3, 0) if h or a or b
    ]
    for peer in lon_peers + lat_peers:
        pl.semaphore_signal(bar, inc=1, device_id=peer, device_id_type=MESH)
    for load in loads:
        load.start()

    lane = iota((16, 128), 1)
    row = iota((16, 128), 0)
    sub8 = iota((8, 128), 0)
    big_lane = iota((128, 128), 1)
    big_row = iota((128, 128), 0)

    KAP[71] = jnp.zeros((16, 128), F32)
    ZP[...] = jnp.zeros((128, 128), F32)

    perm_lane = (big_lane & 15) * 8 + big_lane // 16
    perm_row = (big_row & 15) * 8 + big_row // 16
    rows_f = big_row.astype(F32)
    lanes_f = big_lane.astype(F32)

    def total(mask, values, axis):
        kept = jnp.sum(jnp.where(mask, values, 0.0), axis=axis, keepdims=True)
        return jnp.broadcast_to(kept, (128, 128))

    def remote(src, dst, send, recv, dev):
        return pltpu.make_async_remote_copy(
            src_ref=src, dst_ref=dst, send_sem=send, recv_sem=recv,
            device_id=dev, device_id_type=MESH,
        )

    def edge_copies(s):
        return (
            remote(
                F.at[s, :, :, pl.ds(0, 1), :], F.at[s, :, :, pl.ds(16, 1), :],
                ns.at[s], nr.at[s], south,
            ),
            remote(ES.at[s], EE.at[s], es.at[s], er.at[s], west),
        )

    zero = jnp.zeros((16, 128), F32)
    loads[0].wait()
    for t in range(2):
        E01[t] = jnp.where(lane == 0, F[0, t, 0, 0:16, :], pltpu.roll(F[0, t, 1, 0:16, :], 1, 1))
    loads[1].wait()
    pl.semaphore_wait(bar, 30)
    early = [
        remote(src, dst, ts.at[i], tr.at[i], dev)
        for i, (src, dst, dev) in enumerate((
            (E01, E01N, west),
            (F.at[0, :, pl.ds(0, 2), pl.ds(0, 1), :], F.at[0, :, pl.ds(0, 2), pl.ds(16, 1), :], south),
            (CO.at[0], CZE, west),
            (CO.at[1, pl.ds(0, 8)], CMN, south),
        ))
    ]
    for peer in lat_peers:
        pl.semaphore_signal(stage, inc=1, device_id=peer, device_id_type=MESH)
    for copy in early:
        copy.start()

    loads[2].wait()
    p_row = jnp.broadcast_to(PT[...], (128, 128))
    t_row, l_row = (p_row // 128).astype(F32), (p_row & 127).astype(F32)
    t_col = total(big_row == big_lane, t_row, 1)

    def sent(order):
        target = total(big_row == order, t_col, 0)
        slot = total((t_col == target) & (big_row < order), 1.0, 0)
        return target, slot

    t_send, k_send = sent(perm_lane)
    t_rev, k_rev = sent(big_lane ^ 7)
    t_from = total(big_lane == perm_row, t_row, 1)
    l_from = total(big_lane == perm_row, l_row, 1)
    KM[...] = total((t_row == t_from) & (l_row < l_from), 1.0, 1)
    loads[3].wait()
    loads[4].wait()
    a1 = CP[...] * KAP[0]
    a0 = CP[...] - a1
    ST[0:16] = a0
    ST[16:32] = a1
    ST[32:40] = jnp.where(
        sub8 == 0, t_send[0:8],
        jnp.where(sub8 == 1, k_send[0:8], jnp.where(sub8 == 2, t_rev[0:8], k_rev[0:8])),
    )
    CF[0] = 1.0 - CO[0] - CO[1]
    for half in (0, 128):
        for k in (0, 1):
            OHP[128 * k:128 * k + 128, half:half + 128] = jnp.where(
                (t_send == rows_f) & (k_send == float(k)), 1.0, 0.0
            ).astype(BF16)
    for load in loads[5:]:
        load.wait()
    CF[1] = MK[...].astype(F32)

    def pack_level(k, edges):
        return tuple(
            jnp.where(lane == k, pltpu.roll(F[0, t, k, 0:16, :], k, 1), edges[t]) for t in range(2)
        )

    packed = lax.fori_loop(0, 72, pack_level, (zero, zero))
    ES[0, 0] = packed[0]
    ES[0, 1] = packed[1]

    later = [
        remote(src, dst, ts.at[4 + i], tr.at[4 + i], dev)
        for i, (src, dst, dev) in enumerate((
            (ES.at[0], EE.at[0], west),
            (F.at[0, :, pl.ds(2, 70), pl.ds(0, 1), :], F.at[0, :, pl.ds(2, 70), pl.ds(16, 1), :], south),
            (ST, STW, east),
            (ST, STS, north),
        ))
    ]
    for copy in later:
        copy.start()
    for copy in early:
        copy.wait()
    has_north = jnp.where(lat < 7, 1.0, 0.0)
    CF[4] = jnp.broadcast_to(CZE[:, 0:1], (16, 128))
    CMS[0:16] = CO[1]
    CMS[16:24] = jnp.broadcast_to(CMN[0:1], (8, 128)) * has_north
    CF[5] = CMS[1:17]

    def edge_columns(ref):
        return [ref[t] * CF[4] for t in range(2)]

    def advected(s, t, k, columns):
        f, f_north = F[s, t, k, 0:16, :], F[s, t, k, 1:17, :]
        column = pltpu.roll(columns[t], 127 - k, 1)
        east_next = jnp.where(lane == 127, column, pltpu.roll(CO[0] * f, 127, 1))
        return CF[0] * f + east_next + CF[5] * f_north

    def own_slots(own):
        parts = []
        for c in range(8):
            first = pltpu.roll(own[0], (128 - 16 * c) & 127, 1)
            second = pltpu.roll(own[1], (144 - 16 * c) & 127, 1)
            parts.append(jnp.where(lane < 16, first, jnp.where(lane < 32, second, 0.0)))
        tiles = jnp.concatenate(parts, axis=0)
        both = dot(OHP[...], jnp.concatenate(halves(tiles), axis=0))
        return both[0:128] + pltpu.roll(both[128:256], 64, 1)

    def pack_first():
        columns = edge_columns(E01N)
        own = []
        for t in range(2):
            own.append(ST[0:16] * advected(0, t, 0, columns) + ST[16:32] * advected(0, t, 1, columns))
        SB[0, 0] = own_slots(own)

    def pack(s, surfaces):
        cz, cm = CO[0], CO[1]
        edge = jnp.zeros((16, 128), F32)
        own, north_parts = [], []
        for t in range(2):
            f0, f1 = surfaces[t], F[s, t, 1, 0:16, :]
            z0, z1, m0, m1 = cz * f0, cz * f1, cm * f0, cm * f1
            value = jnp.zeros((16, 128), F32)
            for c, f, zf, mf in ((ST[0:16], f0, z0, m0), (ST[16:32], f1, z1, m1)):
                east_next = jnp.where(lane == 127, 0.0, pltpu.roll(zf, 127, 1))
                north_next = jnp.where(row == 15, 0.0, pltpu.roll(mf, 15, 0))
                value += c * (CF[0] * f + east_next + north_next)
            own.append(value)
            to_south = jnp.broadcast_to((ROWS[0] * m0[0:8] + ROWS[1] * m1[0:8])[0:1], (8, 128))
            if t:
                to_south = pltpu.roll(to_south, 16, 1)
            north_parts.append(pltpu.roll(to_south, 16, 1, stride=16, stride_axis=0))
            to_west = CF[2] * z0 + CF[3] * z1
            edge = jnp.where(lane == 15 + 16 * t, pltpu.roll(to_west, 15 + 16 * t, 1), edge)
        lanes = iota((8, 128), 1)
        both = jnp.where(lanes < 16, north_parts[0], jnp.where(lanes < 32, north_parts[1], 0.0))
        north_tiles = pltpu.roll(both, 32, 1)
        added = jnp.concatenate(
            [north_tiles, pltpu.roll(north_tiles, 64, 1), edge, pltpu.roll(edge, 64, 1), zero], axis=0
        )
        extra = jnp.concatenate(halves(added), axis=0)
        SB[s, 0] = own_slots(own) + dot(OHX[0:128], extra)
        SB[s, 1] = dot(OHX[128:256], extra)

    def send(s, count):
        planes = pl.ds(0, count)
        for a, b, c, d in OFFSETS:
            to_lat = (x_lo ^ a) * 4 + ((y + b) & 3)
            to_lon = ((z + c) & 7) * 2 + (core ^ d)
            remote(
                SB.at[s, planes, pl.ds(to_lat * 16 + to_lon, 1), :],
                RB.at[s, planes, pl.ds(me, 1), :],
                xs.at[s], xr.at[s], (1 - mp, to_lat, to_lon),
            ).start()

    def deep_copy():
        return pltpu.make_async_copy(
            F.at[STEPS, :, pl.ds(1, 71), pl.ds(0, 16), :], out.at[0, :, pl.ds(1, 71)], osem.at[0]
        )

    def received_surface(s):
        plane = RB[s, 0]
        parts = [plane, pltpu.roll(plane, 96, 1), RB[s, 1]]
        gathered = dot(LR[...], jnp.concatenate([half for part in parts for half in halves(part)], axis=0))
        tiles = jnp.where(KM[...] == 0.0, gathered, pltpu.roll(gathered, 64, 1))
        out_0, out_1 = zero, zero
        for c in range(8):
            moved = pltpu.roll(tiles[16 * c:16 * c + 16], 16 * c, 1)
            out_0 = jnp.where(lane // 16 == c, moved, out_0)
            out_1 = jnp.where(lane // 16 == (c + 1) % 8, moved, out_1)
        return out_0, pltpu.roll(out_1, 112, 1)

    pack_first()
    blank = pltpu.make_async_copy(ZP, RB.at[0, 1], xr.at[0])
    blank.start()
    pl.semaphore_wait(stage, 15)
    send(0, 1)
    own_rows = (t_from == lanes_f)
    north_rows = (l_from >= 120.0) & (lanes_f == t_from + 16.0)
    t_int = t_from.astype(jnp.int32)
    t_east = (t_int - (t_int & 15)) + ((t_int + 1) & 15)
    east_rows = ((l_from.astype(jnp.int32) & 7) == 7) & (big_lane == t_east)
    for i, rows in enumerate((own_rows, own_rows, north_rows, north_rows, east_rows, east_rows)):
        LR[:, 128 * i:128 * i + 128] = jnp.where(rows, 1.0, 0.0).astype(BF16)

    for copy in later:
        copy.wait()
    spread = lambda x: jnp.broadcast_to(x, (128, 128))

    def shifted_slots(ref, first, shifts, start, count):
        t_all, k_all = spread(ref[first:first + 1]), spread(ref[first + 1:first + 2])
        hit = jnp.zeros((128, 128), F32)
        for k in (0, 1):
            for half in (0, 64):
                shift = (shifts[k] + half) & 127
                inside = (big_lane >= start + count * k + half) & (big_lane < start + count * (k + 1) + half)
                found = (pltpu.roll(t_all, shift, 1) == rows_f) & (pltpu.roll(k_all, shift, 1) == float(k))
                hit = jnp.where(inside & found, 1.0, hit)
        return hit.astype(BF16)

    OHX[0:128] = shifted_slots(STS, 34, (8, 16), 0, 8)
    OHX[128:256] = shifted_slots(STW, 32, (32, 48), 16, 16)
    has_south = jnp.where(lat > 0, 1.0, 0.0)
    ROWS[0] = jnp.broadcast_to(STS[15:16], (8, 128)) * has_south
    ROWS[1] = jnp.broadcast_to(STS[31:32], (8, 128)) * has_south
    CF[2] = jnp.broadcast_to(STW[0:16, 127:128], (16, 128))
    CF[3] = jnp.broadcast_to(STW[16:32, 127:128], (16, 128))

    def step(s, carry):
        columns = edge_columns(EE.at[s])

        def block(b, state):
            first = b * BLOCK
            above = [
                [advected(s, t, jnp.minimum(first + j + 1, 71), columns) for j in range(BLOCK)]
                for t in range(2)
            ]
            new = []
            for t in range(2):
                here, flux_below, edge = state[t]
                for j in range(BLOCK):
                    flux = KAP[first + j] * (above[t][j] - here)
                    mixed = here + flux - flux_below
                    F[s + 1, t, first + j, 0:16, :] = mixed
                    edge = jnp.where(lane == first + j, pltpu.roll(mixed, first + j, 1), edge)
                    here, flux_below = above[t][j], flux
                new.append((here, flux_below, edge))
            return tuple(new)

        state = tuple((advected(s, t, 0, columns), zero, zero) for t in range(2))
        state = lax.fori_loop(0, 72 // BLOCK, block, state)

        @pl.when(s == STEPS - 1)
        def _():
            deep_copy().start()

        pltpu.make_async_copy(RB.at[s], RB.at[s], xr.at[s]).wait()
        received = received_surface(s)
        surfaces = []
        for t in range(2):
            mixed = F[s + 1, t, 0, 0:16, :]
            surfaces.append(mixed + CF[1] * (received[t] - CP[...] * mixed))

        @pl.when(s < STEPS - 1)
        def _():
            for t in range(2):
                F[s + 1, t, 0, 0:16, :] = surfaces[t]
                ES[s + 1, t] = jnp.where(lane == 0, surfaces[t], state[t][2])
            copies = edge_copies(s + 1)
            for copy in copies:
                copy.start()
            pack(s + 1, surfaces)
            send(s + 1, 2)
            for copy in copies:
                copy.wait()

        @pl.when(s == STEPS - 1)
        def _():
            for t in range(2):
                out[0, t, 0] = surfaces[t]

        return carry

    lax.fori_loop(0, STEPS, step, 0)
    for s in range(STEPS):
        gone = SB.at[s] if s else SB.at[s, 0]
        pltpu.make_async_copy(gone, gone, xs.at[s]).wait()
    deep_copy().wait()


def local(adjoint, courant, diffusivity, coupling, partner, mask):
    any_space = pl.BlockSpec(memory_space=pl.ANY)
    vmem = pltpu.VMEM
    dma = pltpu.SemaphoreType.DMA
    return pl.pallas_call(
        kernel,
        out_shape=vmem(adjoint.shape, F32),
        in_specs=[any_space] * 6,
        out_specs=pl.BlockSpec(memory_space=vmem),
        scratch_shapes=[
            vmem((STEPS + 1, 2, 72, 24, 128), F32),
            vmem((2, 16, 128), F32),
            vmem((72, 16, 128), F32),
            vmem((16, 128), F32),
            vmem((1, 128), jnp.int32),
            vmem((16, 128), jnp.int32),
            vmem((40, 128), F32),
            vmem((40, 128), F32),
            vmem((40, 128), F32),
            vmem((16, 128), F32),
            vmem((8, 128), F32),
            vmem((24, 128), F32),
            vmem((STEPS, 2, 16, 128), F32),
            vmem((STEPS, 2, 16, 128), F32),
            vmem((2, 16, 128), F32),
            vmem((2, 16, 128), F32),
            vmem((STEPS, 2, 128, 128), F32),
            vmem((STEPS, 2, 128, 128), F32),
            vmem((256, 256), BF16),
            vmem((256, 128), BF16),
            vmem((128, 768), BF16),
            vmem((128, 128), F32),
            vmem((6, 16, 128), F32),
            vmem((2, 8, 128), F32),
            vmem((128, 128), F32),
            dma((8,)),
            dma((1,)),
            dma((STEPS,)),
            dma((STEPS,)),
            dma((STEPS,)),
            dma((STEPS,)),
            dma((STEPS,)),
            dma((STEPS,)),
            dma((8,)),
            dma((8,)),
            pltpu.SemaphoreType.REGULAR,
        ],
        compiler_params=pltpu.CompilerParams(collective_id=0, has_side_effects=True),
    )(adjoint, courant, diffusivity, coupling, partner, mask)


def solution(mesh):
    placed = (
        P("mp", None, None, "lat", "lon"),
        P("mp", None, "lat", "lon"),
        P("mp", None, "lat", "lon"),
        P("mp", "lat", "lon"),
        P("mp", ("lat", "lon")),
        P("mp", "lat", "lon"),
    )
    return jax.shard_map(
        local,
        mesh=mesh,
        in_specs=placed,
        out_specs=P("mp", None, None, "lat", "lon"),
        check_vma=False,
    )
```
